32 devices in a mesh: seq: 8 (over z, x), head: 4 (over y, core).
Axes of the slice: x: 2, y: 2, z: 4, core: 2. Of those that a mesh axis runs over, the one named last changes fastest.
Arguments:
- queries: bfloat16 [1024, 4096], P(('seq', 'head')), may hold values from -0.5 to 0.5
- keys: bfloat16 [1024, 4096], P(('seq', 'head')), may hold values from -0.5 to 0.5
- values: bfloat16 [1024, 4096], P(('seq', 'head')), may hold values from -6 to 6
- grad_out: bfloat16 [1024, 4096], P(('seq', 'head')), may hold values from -6 to 6
- gates: float32 [1024, 32], P('seq', 'head'), may hold values from -1.5 to 0, as said below
Outputs:
- grad_queries: bfloat16 [1024, 4096], P('seq', 'head')
- grad_keys: bfloat16 [1024, 4096], P('seq', 'head')
- grad_values: bfloat16 [1024, 4096], P('seq', 'head')
The draws below stay inside these ranges and needn't reach their ends.
Inputs may be any that keep to these rules, and one draw needn't show every extreme that they name: gates are negative.
All inputs are finite; a program needn't handle non-finite values.
Results may differ from the reference program's by a relative error of at most 0.0058.
Values may be sent and summed in bfloat16 or wider, within the bound.
A program may use at most 128 MiB of HBM per device.

```python
import math
import jax
import jax.numpy as jnp
from jax import lax

HEAD_COUNT = 32
DH = 128
TOK_DEV = 128
TOKEN_COUNT = 1024
N_SEQ = 8


def draw_gates(key, part):
    pick_key, fast_key, slow_key, rough_key, location_random_key, depth_random_key = jax.random.split(key, 6)
    fast_share = 0.5
    fast_heads = jax.random.uniform(pick_key, (HEAD_COUNT,), jnp.float32) < fast_share
    fast_rate = jnp.exp(jax.random.uniform(fast_key, (HEAD_COUNT,), jnp.float32, math.log(1.0 / 50.0), math.log(1.0 / 30.0)))
    slow_rate = jnp.exp(jax.random.uniform(slow_key, (HEAD_COUNT,), jnp.float32, math.log(0.05 / TOKEN_COUNT), math.log(0.6 / TOKEN_COUNT)))
    per_head_rate = jnp.where(fast_heads, fast_rate, slow_rate)
    jaggedness = jax.random.uniform(rough_key, (TOKEN_COUNT, HEAD_COUNT), jnp.float32, 0.5, 1.5)
    spike_locations = jax.random.randint(location_random_key, (2, HEAD_COUNT), 0, TOKEN_COUNT)
    spike_depth = jnp.log(jax.random.uniform(depth_random_key, (2, HEAD_COUNT), jnp.float32, 0.5, 0.8))
    position_indices = jnp.arange(TOKEN_COUNT)[:, None]
    spike_events = jnp.where(position_indices == spike_locations[0][None, :], spike_depth[0][None, :], 0.0)
    spike_events = spike_events + jnp.where(position_indices == spike_locations[1][None, :], spike_depth[1][None, :], 0.0)
    return (-per_head_rate[None, :] * jaggedness + spike_events).astype(jnp.float32)


def block_levels(own_key, extent, pieces, smallest, top_value):
    factor_of = 1.0
    for dim, blocks in pieces:
        heights = jax.random.uniform(jax.random.fold_in(jax.random.fold_in(own_key, 6), dim), (blocks,), jnp.float32, smallest / len(pieces), top_value / len(pieces))
        factor_of = factor_of * jnp.repeat(jnp.exp(heights), extent[dim] // blocks).reshape((-1,) + (1,) * (len(extent) - 1 - dim))
    return factor_of


def bell_draw(own_key, shape, width, limit, cuts=(), dtype=jnp.bfloat16):
    gain = block_levels(own_key, shape, cuts, -0.22, 0.18) if cuts else 1.0
    values = jax.random.normal(own_key, shape, jnp.float32) * width * gain
    return jnp.minimum(jnp.maximum(values, -limit), limit).astype(dtype)


def setup_inputs(seed: int = 0) -> dict:
    seeds = jax.random.split(jax.random.key(seed), 6)
    return {
        "queries": bell_draw(seeds[0], (TOKEN_COUNT, HEAD_COUNT * DH), DH ** -0.5, 0.5, ((0, 32),)),
        "keys": bell_draw(seeds[1], (TOKEN_COUNT, HEAD_COUNT * DH), DH ** -0.5, 0.5, ((0, 32),)),
        "values": bell_draw(seeds[2], (TOKEN_COUNT, HEAD_COUNT * DH), 1.0, 6.0, ((0, 32),)),
        "grad_out": bell_draw(seeds[3], (TOKEN_COUNT, HEAD_COUNT * DH), 1.0, 6.0, ((0, 32),)),
        "gates": draw_gates(jax.random.fold_in(seeds[5], 71), 0),
    }


HIGHEST_PRECISION = lax.Precision.HIGHEST

def decay_parts(gate_rows):
    cumulated = jnp.cumsum(gate_rows, axis=0)
    block_end = cumulated[-1]
    by_head = cumulated.T
    position_indices = jnp.arange(cumulated.shape[0])
    causal = position_indices[:, None] >= position_indices[None, :]
    log_gaps = jnp.where(causal[None], by_head[:, :, None] - by_head[:, None, :], 0.0)
    decay_table = jnp.where(causal[None], jnp.exp(log_gaps), 0.0)
    return (cumulated, block_end, decay_table)

def reference(queries, keys, values, grad_out, gates):
    block_shape = (N_SEQ, TOK_DEV, HEAD_COUNT, DH)
    query_blocks = queries.reshape(block_shape)
    key_blocks = keys.reshape(block_shape)
    value_blocks = values.reshape(block_shape)
    grad_blocks = grad_out.reshape(block_shape)
    gate_blocks = gates.reshape(N_SEQ, TOK_DEV, HEAD_COUNT)

    def forward_block(carry, inputs):
        prefix_state, prefix_norm = carry
        query_rows, key_rows, value_rows, grad_rows, gate_rows = inputs
        cumulated, block_end, decay_table = decay_parts(gate_rows)
        growth = jnp.exp(cumulated)
        fade_out = jnp.exp(block_end[None, :] - cumulated)
        carry_gain = jnp.exp(block_end)
        norm_total = growth * prefix_norm[None, :] + lax.optimization_barrier(jnp.sum(decay_table, axis=2)).T
        inverse_root = lax.rsqrt(norm_total)
        scaled = (grad_rows.astype(jnp.float32) * inverse_root[:, :, None]).astype(jnp.bfloat16)
        mixing = jnp.einsum('the,she->hts', grad_rows.astype(jnp.float32), value_rows.astype(jnp.float32))
        weighted = (mixing * decay_table * inverse_root.T[:, :, None]).astype(jnp.bfloat16)
        prefix_low = prefix_state.astype(jnp.bfloat16)
        grad_q = jnp.einsum('hts,shd->thd', weighted.astype(jnp.float32), key_rows.astype(jnp.float32))
        grad_q = grad_q + growth[:, :, None] * jnp.einsum('the,hde->thd', scaled.astype(jnp.float32), prefix_low.astype(jnp.float32))
        key_fade = key_rows.astype(jnp.float32) * fade_out[:, :, None]
        local_state = jnp.einsum('thd,the->hde', key_fade, value_rows.astype(jnp.float32), precision=HIGHEST_PRECISION)
        next_state = carry_gain[:, None, None] * prefix_state + local_state
        next_norm = carry_gain * prefix_norm + lax.optimization_barrier(jnp.sum(fade_out, axis=0))
        return ((next_state, next_norm), (grad_q.astype(jnp.bfloat16), scaled, inverse_root))
    start_state = jnp.zeros((HEAD_COUNT, DH, DH), jnp.float32)
    start_norm = jnp.zeros((HEAD_COUNT,), jnp.float32)
    unused, (grad_q_blocks, scaled_blocks, root_blocks) = lax.scan(forward_block, (start_state, start_norm), (query_blocks, key_blocks, value_blocks, grad_blocks, gate_blocks))

    def backward_block(later_state, inputs):
        query_rows, key_rows, value_rows, grad_rows, gate_rows, scaled, inverse_root = inputs
        cumulated, block_end, decay_table = decay_parts(gate_rows)
        growth = jnp.exp(cumulated)
        fade_out = jnp.exp(block_end[None, :] - cumulated)
        carry_gain = jnp.exp(block_end)
        query_wide = query_rows.astype(jnp.float32)
        key_wide = key_rows.astype(jnp.float32)
        value_wide = value_rows.astype(jnp.float32)
        scaled_wide = scaled.astype(jnp.float32)
        mixing = jnp.einsum('the,she->hts', grad_rows.astype(jnp.float32), value_wide)
        weighted = (mixing * decay_table * inverse_root.T[:, :, None]).astype(jnp.bfloat16)
        affinity = (jnp.einsum('thd,shd->hts', query_wide, key_wide) * decay_table).astype(jnp.bfloat16)
        later_low = later_state.astype(jnp.bfloat16).astype(jnp.float32)
        grad_k = jnp.einsum('hts,thd->shd', weighted.astype(jnp.float32), query_wide)
        grad_k = grad_k + fade_out[:, :, None] * jnp.einsum('she,hde->shd', value_wide, later_low)
        grad_v = jnp.einsum('hts,the->she', affinity.astype(jnp.float32), scaled_wide)
        grad_v = grad_v + fade_out[:, :, None] * jnp.einsum('shd,hde->she', key_wide, later_low)
        reach = jnp.einsum('thd,the->hde', query_wide * growth[:, :, None], scaled_wide, precision=HIGHEST_PRECISION)
        next_later = carry_gain[:, None, None] * later_state + reach
        return (next_later, (grad_k.astype(jnp.bfloat16), grad_v.astype(jnp.bfloat16)))
    unused_later, (grad_k_blocks, grad_v_blocks) = lax.scan(backward_block, jnp.zeros((HEAD_COUNT, DH, DH), jnp.float32), (query_blocks, key_blocks, value_blocks, grad_blocks, gate_blocks, scaled_blocks, root_blocks), reverse=True)
    flat_shape = (TOKEN_COUNT, HEAD_COUNT * DH)
    return (grad_q_blocks.reshape(flat_shape), grad_k_blocks.reshape(flat_shape), grad_v_blocks.reshape(flat_shape))
```

```python
import functools

import jax
import jax.numpy as jnp
from jax import lax
from jax.experimental import pallas as pl
from jax.experimental.pallas import tpu as pltpu
from jax.sharding import PartitionSpec as P

HEAD_COUNT = 32
DH = 128
SLOW = 4
CHUNK_HEADS = 2
LAG = 1
TAIL = 1

MESH = pl.DeviceIdType.MESH
F32 = jnp.float32
BF16 = jnp.bfloat16
EXACT = lax.Precision.HIGHEST


def dot_nn(x, y):
    return lax.dot_general(x, y, (((1,), (0,)), ((), ())), preferred_element_type=F32)


def dot_nt(x, y):
    return lax.dot_general(x, y, (((1,), (1,)), ((), ())), preferred_element_type=F32)


def dot_tn(x, y):
    return lax.dot_general(x, y, (((0,), (0,)), ((), ())), preferred_element_type=F32)


def kernel(
    seq_size, head_size,
    q_ref, k_ref, v_ref, g_ref, gates_ref,
    gq_ref, gk_ref, gv_ref,
    rows, ends, gain, table, grow, fade, inner, scaled_ref,
    local, reach, part_q, part_k, part_v,
    y_send, y_recv, n_send, n_recv, zp_send, zp_recv, zn_send, zn_recv,
    zgain,
    a2a_ssem, a2a_rsem, end_ssem, end_rsem,
    y_ssem, y_rsem, n_ssem, n_rsem, zp_ssem, zp_rsem, zn_ssem, zn_rsem,
):
    S, H = seq_size, head_size
    A = SLOW
    B = S // A
    RD = q_ref.shape[0]
    T = RD * H
    CW = q_ref.shape[1] // H
    NH = CW // DH
    HC = CHUNK_HEADS
    NC = NH // HC
    CC = HC * DH
    me_s = lax.axis_index("seq")
    me_h = lax.axis_index("head")
    a = me_s // B
    b = me_s % B
    lo = a * B
    hi = lo + B

    barrier = pltpu.get_barrier_semaphore()
    for r in range(1, H):
        pl.semaphore_signal(
            barrier, inc=1, device_id={"head": (me_h + r) % H}, device_id_type=MESH
        )

    @pl.loop(1, S)
    def _(r):
        pl.semaphore_signal(
            barrier, inc=1, device_id={"seq": (me_s + r) % S}, device_id_type=MESH
        )

    t_at = lax.broadcasted_iota(jnp.int32, (T, T), 0)
    s_at = lax.broadcasted_iota(jnp.int32, (T, T), 1)
    causal = t_at >= s_at
    tri = jnp.where(causal, 1.0, 0.0).astype(F32)
    gates = gates_ref[...]
    c_col = lax.dot_general(
        tri, gates, (((1,), (0,)), ((), ())), precision=EXACT, preferred_element_type=F32
    )
    c_row = c_col.T
    e_col = c_row[:, T - 1 : T]
    norm_col = jnp.sum(jnp.exp(e_col - c_row), axis=1, keepdims=True)
    ends[me_s, 0] = jnp.broadcast_to(norm_col, (NH, DH))
    ends[me_s, 1] = jnp.broadcast_to(e_col, (NH, DH))

    pl.semaphore_wait(barrier, (H - 1) + (S - 1))

    def end_copy(r, source, target):
        return pltpu.make_async_remote_copy(
            src_ref=ends.at[source],
            dst_ref=ends.at[source],
            send_sem=end_ssem.at[r - 1],
            recv_sem=end_rsem.at[r - 1],
            device_id={"seq": target},
            device_id_type=MESH,
        )

    @pl.loop(1, S)
    def _(r):
        end_copy(r, me_s, (me_s + r) % S).start()

    in_refs = (q_ref, k_ref, v_ref, g_ref)

    def a2a_copy(ch, r, t, source, target):
        return pltpu.make_async_remote_copy(
            src_ref=in_refs[t].at[:, pl.ds(pl.multiple_of(target * CW + ch * CC, CC), CC)],
            dst_ref=rows.at[
                t,
                pl.ds(pl.multiple_of(source * RD, RD), RD),
                pl.ds(pl.multiple_of(ch * CC, CC), CC),
            ],
            send_sem=a2a_ssem.at[ch, r - 1, t],
            recv_sem=a2a_rsem.at[ch, r - 1, t],
            device_id={"head": target},
            device_id_type=MESH,
        )

    @pl.loop(0, NC)
    def _(ch):
        for t in (1, 2, 0, 3):
            for r in range(1, H):
                a2a_copy(ch, r, t, me_h, (me_h + r) % H).start()

    own_rows = pl.ds(pl.multiple_of(me_h * RD, RD), RD)
    own_cols = pl.ds(pl.multiple_of(me_h * CW, CW), CW)
    for t in range(4):
        rows[t, own_rows, :] = in_refs[t][:, own_cols]

    @pl.when(a == 0)
    def _():
        y_recv[...] = jnp.zeros_like(y_recv)

    @pl.when(a == A - 1)
    def _():
        n_recv[...] = jnp.zeros_like(n_recv)

    for h in range(NH):
        col = c_col[:, h : h + 1]
        row = c_row[h : h + 1, :]
        decay = jnp.where(causal, jnp.exp(jnp.where(causal, col - row, 0.0)), 0.0)
        table[h] = decay
        grow[h] = jnp.broadcast_to(jnp.exp(col), (T, DH))
        fade[h] = jnp.broadcast_to(jnp.exp(c_col[T - 1 : T, h : h + 1] - col), (T, DH))
        inner[h] = jnp.broadcast_to(jnp.sum(decay, axis=1, keepdims=True), (T, DH))

    @pl.loop(1, S)
    def _(r):
        end_copy(r, (me_s + S - r) % S, me_s).wait_recv()

    zero = jnp.zeros((NH, DH), F32)

    def one_block(m, carry):
        pre, suf, norm = carry
        end = ends[m, 1]
        pre = pre + jnp.where((m >= lo) & (m < me_s), 1.0, 0.0) * end
        suf = suf + jnp.where((m > me_s) & (m < hi), 1.0, 0.0) * end
        earlier = jnp.where(m < me_s, 1.0, 0.0)
        norm = earlier * (norm * jnp.exp(end) + ends[m, 0]) + (1.0 - earlier) * norm
        return (pre, suf, norm)

    pre, suf, norm = lax.fori_loop(0, S, one_block, (zero, zero, zero))
    gain[0] = jnp.exp(pre)
    gain[1] = jnp.exp(suf)
    gain[2] = jnp.exp(pre + suf + ends[me_s, 1])
    gain[3] = norm

    @pl.loop(0, B - 1)
    def _(p):
        other = lo + (b + p + 1) % B

        def one_end(m, carry):
            pre, suf, between = carry
            end = ends[m, 1]
            pre = pre + jnp.where((m >= lo) & (m < other), 1.0, 0.0) * end
            suf = suf + jnp.where((m > other) & (m < hi), 1.0, 0.0) * end
            inside = (m > jnp.minimum(me_s, other)) & (m < jnp.maximum(me_s, other))
            between = between + jnp.where(inside, 1.0, 0.0) * end
            return (pre, suf, between)

        pre, suf, between = lax.fori_loop(0, S, one_end, (zero, zero, zero))
        zgain[p, 0] = jnp.exp(pre)
        zgain[p, 1] = jnp.where(other > me_s, 1.0, 0.0) * jnp.exp(between)
        zgain[p, 2] = jnp.exp(suf)
        zgain[p, 3] = jnp.where(other < me_s, 1.0, 0.0) * jnp.exp(between)

    def chain_copy(send, recv, ssem, rsem, m, target):
        return pltpu.make_async_remote_copy(
            src_ref=send.at[m],
            dst_ref=recv.at[m],
            send_sem=ssem.at[m],
            recv_sem=rsem.at[m],
            device_id={"seq": target},
            device_id_type=MESH,
        )

    def y_copy(m, target):
        return chain_copy(y_send, y_recv, y_ssem, y_rsem, m, target)

    def n_copy(m, target):
        return chain_copy(n_send, n_recv, n_ssem, n_rsem, m, target)

    def z_copy(send, recv, ssem, rsem, p, m, target):
        return pltpu.make_async_remote_copy(
            src_ref=send.at[p, m],
            dst_ref=recv.at[p, m],
            send_sem=ssem.at[p, m],
            recv_sem=rsem.at[p, m],
            device_id={"seq": target},
            device_id_type=MESH,
        )

    def zp_copy(p, m, target):
        return z_copy(zp_send, zp_recv, zp_ssem, zp_rsem, p, m, target)

    def zn_copy(p, m, target):
        return z_copy(zn_send, zn_recv, zn_ssem, zn_rsem, p, m, target)

    def peer(p):
        return lo + (b + p + 1) % B

    def source_peer(p):
        return lo + (b + B - p - 1) % B

    up = (me_s + B) % S
    down = (me_s + S - B) % S

    def weight(index, h):
        return gain[index, pl.ds(h, 1), :]

    def columns(h):
        return pl.ds(pl.multiple_of(h * DH, DH), DH)

    def arrive(m):
        for r in range(1, H):
            for t in range(4):
                a2a_copy(m, r, t, (me_h + H - r) % H, me_h).wait_recv()

    def states(m):
        for j in range(HC):
            h = m * HC + j
            at = columns(h)
            growth = grow[h]
            inverse = lax.rsqrt(growth * weight(3, h) + inner[h])
            inner[h] = inverse
            scaled = (rows[3, :, at].astype(F32) * inverse).astype(BF16)
            scaled_ref[h] = scaled
            key_fade = (rows[1, :, at].astype(F32) * fade[h]).astype(BF16)
            local[h] = dot_tn(key_fade, rows[2, :, at])
            query_growth = (rows[0, :, at].astype(F32) * growth).astype(BF16)
            reach[h] = dot_tn(query_growth, scaled)

    def within(m):
        for j in range(HC):
            h = m * HC + j
            at = columns(h)
            q, k, v, g = rows[0, :, at], rows[1, :, at], rows[2, :, at], rows[3, :, at]
            decay = table[h]
            weighted = (dot_nt(g, v) * decay * inner[h]).astype(BF16)
            affinity = (dot_nt(q, k) * decay).astype(BF16)
            part_q[h] = dot_nn(weighted, k)
            part_k[h] = dot_tn(weighted, q)
            part_v[h] = dot_tn(affinity, scaled_ref[h])

    def hop_up(m):
        @pl.when(a > 0)
        def _():
            y_copy(m, up).wait_recv()

        @pl.when(a < A - 1)
        def _():
            for j in range(HC):
                h = m * HC + j
                y_send[m, j] = (
                    weight(1, h) * local[h] + weight(2, h) * y_recv[m, j].astype(F32)
                ).astype(BF16)
            y_copy(m, up).start()

        @pl.loop(0, B - 1)
        def _(p):
            for j in range(HC):
                h = m * HC + j
                zp_send[p, m, j] = (
                    zgain[p, 0, pl.ds(h, 1), :] * y_recv[m, j].astype(F32)
                    + zgain[p, 1, pl.ds(h, 1), :] * local[h]
                ).astype(BF16)
            zp_copy(p, m, peer(p)).start()

    def hop_down(m):
        @pl.when(a < A - 1)
        def _():
            n_copy(m, down).wait_recv()

        @pl.when(a > 0)
        def _():
            for j in range(HC):
                h = m * HC + j
                n_send[m, j] = (
                    weight(0, h) * reach[h] + weight(2, h) * n_recv[m, j].astype(F32)
                ).astype(BF16)
            n_copy(m, down).start()

        @pl.loop(0, B - 1)
        def _(p):
            for j in range(HC):
                h = m * HC + j
                zn_send[p, m, j] = (
                    zgain[p, 2, pl.ds(h, 1), :] * n_recv[m, j].astype(F32)
                    + zgain[p, 3, pl.ds(h, 1), :] * reach[h]
                ).astype(BF16)
            zn_copy(p, m, peer(p)).start()

    def finish(m):
        @pl.loop(0, B - 1)
        def _(p):
            zp_copy(p, m, source_peer(p)).wait_recv()
            zn_copy(p, m, source_peer(p)).wait_recv()

        for j in range(HC):
            h = m * HC + j
            at = columns(h)
            prefix = weight(0, h) * y_recv[m, j].astype(F32)
            later = weight(1, h) * n_recv[m, j].astype(F32)
            prefix, later = lax.fori_loop(
                0,
                B - 1,
                lambda p, both: (
                    both[0] + zp_recv[p, m, j].astype(F32),
                    both[1] + zn_recv[p, m, j].astype(F32),
                ),
                (prefix, later),
            )
            prefix, later = prefix.astype(BF16), later.astype(BF16)
            gq = part_q[h] + grow[h] * dot_nt(scaled_ref[h], prefix)
            gk = part_k[h] + fade[h] * dot_nt(rows[2, :, at], later)
            gv = part_v[h] + fade[h] * dot_nn(rows[1, :, at], later)
            gq_ref[:, at] = gq.astype(BF16)
            gk_ref[:, at] = gk.astype(BF16)
            gv_ref[:, at] = gv.astype(BF16)

    def guarded(do, m):
        @pl.when((m >= 0) & (m < NC))
        def _():
            do(m)

    @pl.loop(0, NC + LAG * (A - 1) + TAIL)
    def _(n):
        @pl.when(n < NC)
        def _():
            arrive(n)
            states(n)

        guarded(hop_up, n - LAG * a)
        guarded(hop_down, n - LAG * (A - 1 - a))

        @pl.when(n < NC)
        def _():
            within(n)

        guarded(finish, n - LAG * (A - 1) - TAIL)

    @pl.loop(1, S)
    def _(r):
        end_copy(r, me_s, (me_s + r) % S).wait_send()

    @pl.loop(0, NC)
    def _(m):
        for r in range(1, H):
            for t in range(4):
                a2a_copy(m, r, t, me_h, (me_h + r) % H).wait_send()

        @pl.when(a < A - 1)
        def _():
            y_copy(m, up).wait_send()

        @pl.when(a > 0)
        def _():
            n_copy(m, down).wait_send()

        @pl.loop(0, B - 1)
        def _(p):
            zp_copy(p, m, peer(p)).wait_send()
            zn_copy(p, m, peer(p)).wait_send()


def body(seq_size, head_size, queries, keys, values, grad_out, gates):
    S, H = seq_size, head_size
    B = S // SLOW
    RD, width = queries.shape
    T = RD * H
    CW = width // H
    NH = CW // DH
    HC = CHUNK_HEADS
    NC = NH // HC
    square = (NH, T, DH)
    state = (NH, DH, DH)
    message = (NC, HC, DH, DH)
    vmem = pltpu.VMEM
    dma = pltpu.SemaphoreType.DMA
    whole = pl.BlockSpec(memory_space=pltpu.VMEM)
    out = jax.ShapeDtypeStruct((T, CW), BF16)
    return pl.pallas_call(
        functools.partial(kernel, S, H),
        out_shape=(out, out, out),
        in_specs=[whole] * 5,
        out_specs=(whole, whole, whole),
        scratch_shapes=[
            vmem((4, T, CW), BF16),
            vmem((S, 2, NH, DH), F32),
            vmem((4, NH, DH), F32),
            vmem((NH, T, T), F32),
            vmem(square, F32),
            vmem(square, F32),
            vmem(square, F32),
            vmem(square, BF16),
            vmem(state, F32),
            vmem(state, F32),
            vmem(square, F32),
            vmem(square, F32),
            vmem(square, F32),
            vmem(message, BF16),
            vmem(message, BF16),
            vmem(message, BF16),
            vmem(message, BF16),
            vmem((B - 1,) + message, BF16),
            vmem((B - 1,) + message, BF16),
            vmem((B - 1,) + message, BF16),
            vmem((B - 1,) + message, BF16),
            vmem((B - 1, 4, NH, DH), F32),
            dma((NC, H - 1, 4)),
            dma((NC, H - 1, 4)),
            dma((S - 1,)),
            dma((S - 1,)),
            dma((NC,)),
            dma((NC,)),
            dma((NC,)),
            dma((NC,)),
            dma((B - 1, NC)),
            dma((B - 1, NC)),
            dma((B - 1, NC)),
            dma((B - 1, NC)),
        ],
        compiler_params=pltpu.CompilerParams(
            collective_id=0,
            has_side_effects=True,
            vmem_limit_bytes=(16 << 20) + (B - 1) * (1 << 20),
        ),
    )(queries, keys, values, grad_out, gates)


def solution(mesh):
    placed = (
        P(("seq", "head"), None),
        P(("seq", "head"), None),
        P(("seq", "head"), None),
        P(("seq", "head"), None),
        P("seq", "head"),
    )
    return jax.shard_map(
        functools.partial(body, mesh.shape["seq"], mesh.shape["head"]),
        mesh=mesh,
        in_specs=placed,
        out_specs=(P("seq", "head"), P("seq", "head"), P("seq", "head")),
        check_vma=False,
    )
```

```python
import functools

import jax
import jax.numpy as jnp
from jax import lax
from jax.experimental import pallas as pl
from jax.experimental.pallas import tpu as pltpu
from jax.sharding import PartitionSpec as P

HEAD_COUNT = 32
DH = 128
SLOW = 4
ROW_HEADS = 2
CHUNK_HEADS = 1
LAG = 2
TAIL = 2

MESH = pl.DeviceIdType.MESH
F32 = jnp.float32
BF16 = jnp.bfloat16
EXACT = lax.Precision.HIGHEST


def dot_nn(x, y):
    return lax.dot_general(x, y, (((1,), (0,)), ((), ())), preferred_element_type=F32)


def dot_nt(x, y):
    return lax.dot_general(x, y, (((1,), (1,)), ((), ())), preferred_element_type=F32)


def dot_tn(x, y):
    return lax.dot_general(x, y, (((0,), (0,)), ((), ())), preferred_element_type=F32)


def kernel(
    seq_size, head_size,
    q_ref, k_ref, v_ref, g_ref, gates_ref,
    gq_ref, gk_ref, gv_ref,
    rows, ends, gain, table, grow, fade, inner, scaled_ref,
    local, reach, part_q, part_k, part_v,
    y_send, y_recv, n_send, n_recv, zp_send, zp_recv, zn_send, zn_recv,
    zgain, out_rows, staged,
    in_sem, out_sem, own_sem, a2a_ssem, a2a_rsem, end_ssem, end_rsem,
    y_ssem, y_rsem, n_ssem, n_rsem, zp_ssem, zp_rsem, zn_ssem, zn_rsem,
):
    S, H = seq_size, head_size
    A = SLOW
    B = S // A
    RD = q_ref.shape[0]
    T = RD * H
    CW = q_ref.shape[1] // H
    NH = CW // DH
    HC = CHUNK_HEADS
    NC = NH // HC
    RC = ROW_HEADS * DH
    PER = ROW_HEADS // HC
    me_s = lax.axis_index("seq")
    me_h = lax.axis_index("head")
    a = me_s // B
    b = me_s % B
    lo = a * B
    hi = lo + B

    def in_copy(t):
        return pltpu.make_async_copy(
            (q_ref, k_ref, v_ref, g_ref)[t], staged.at[t], in_sem.at[t]
        )

    for t in range(4):
        in_copy(t).start()

    barrier = pltpu.get_barrier_semaphore()
    for r in range(1, H):
        pl.semaphore_signal(
            barrier, inc=1, device_id={"head": (me_h + r) % H}, device_id_type=MESH
        )

    @pl.loop(1, S)
    def _(r):
        pl.semaphore_signal(
            barrier, inc=1, device_id={"seq": (me_s + r) % S}, device_id_type=MESH
        )

    t_at = lax.broadcasted_iota(jnp.int32, (T, T), 0)
    s_at = lax.broadcasted_iota(jnp.int32, (T, T), 1)
    causal = t_at >= s_at
    tri = jnp.where(causal, 1.0, 0.0).astype(F32)
    c_row = lax.dot_general(
        gates_ref[...], tri, (((1,), (1,)), ((), ())), precision=EXACT, preferred_element_type=F32
    )
    c_col = c_row.T
    e_col = c_row[:, T - 1 : T]
    norm_col = jnp.sum(jnp.exp(e_col - c_row), axis=1, keepdims=True)
    ends[me_s, 0] = jnp.broadcast_to(norm_col, (NH, DH))
    ends[me_s, 1] = jnp.broadcast_to(e_col, (NH, DH))

    pl.semaphore_wait(barrier, (H - 1) + (S - 1))

    def end_copy(r, source, target):
        return pltpu.make_async_remote_copy(
            src_ref=ends.at[source],
            dst_ref=ends.at[source],
            send_sem=end_ssem.at[r - 1],
            recv_sem=end_rsem.at[r - 1],
            device_id={"seq": target},
            device_id_type=MESH,
        )

    @pl.loop(1, S)
    def _(r):
        end_copy(r, me_s, (me_s + r) % S).start()


    def a2a_copy(ch, r, t, source, target):
        return pltpu.make_async_remote_copy(
            src_ref=staged.at[t, :, pl.ds(pl.multiple_of(target * CW + ch * RC, RC), RC)],
            dst_ref=rows.at[
                t,
                pl.ds(pl.multiple_of(source * RD, RD), RD),
                pl.ds(pl.multiple_of(ch * RC, RC), RC),
            ],
            send_sem=a2a_ssem.at[ch, r - 1, t],
            recv_sem=a2a_rsem.at[ch, r - 1, t],
            device_id={"head": target},
            device_id_type=MESH,
        )

    for t in range(4):
        in_copy(t).wait()

    @pl.loop(0, NH // ROW_HEADS)
    def _(ch):
        for t in (1, 2, 0, 3):
            for r in range(1, H):
                a2a_copy(ch, r, t, me_h, (me_h + r) % H).start()

    own_rows = pl.ds(pl.multiple_of(me_h * RD, RD), RD)
    own_cols = pl.ds(pl.multiple_of(me_h * CW, CW), CW)
    def own_copy(t):
        return pltpu.make_async_copy(
            staged.at[t, :, own_cols], rows.at[t, own_rows, :], own_sem.at[t]
        )

    for t in range(4):
        own_copy(t).start()

    @pl.when(a == 0)
    def _():
        y_recv[...] = jnp.zeros_like(y_recv)

    @pl.when(a == A - 1)
    def _():
        n_recv[...] = jnp.zeros_like(n_recv)

    for h in range(NH):
        col = c_col[:, h : h + 1]
        row = c_row[h : h + 1, :]
        decay = jnp.where(causal, jnp.exp(jnp.where(causal, col - row, 0.0)), 0.0)
        table[h] = decay
        grow[h] = jnp.broadcast_to(jnp.exp(col), (T, DH))
        fade[h] = jnp.broadcast_to(jnp.exp(c_col[T - 1 : T, h : h + 1] - col), (T, DH))
        inner[h] = jnp.broadcast_to(jnp.sum(decay, axis=1, keepdims=True), (T, DH))

    @pl.loop(1, S)
    def _(r):
        end_copy(r, (me_s + S - r) % S, me_s).wait_recv()

    zero = jnp.zeros((NH, DH), F32)

    def one_block(m, carry):
        pre, suf, norm = carry
        end = ends[m, 1]
        pre = pre + jnp.where((m >= lo) & (m < me_s), 1.0, 0.0) * end
        suf = suf + jnp.where((m > me_s) & (m < hi), 1.0, 0.0) * end
        earlier = jnp.where(m < me_s, 1.0, 0.0)
        norm = earlier * (norm * jnp.exp(end) + ends[m, 0]) + (1.0 - earlier) * norm
        return (pre, suf, norm)

    pre, suf, norm = lax.fori_loop(0, S, one_block, (zero, zero, zero))
    gain[0] = jnp.exp(pre)
    gain[1] = jnp.exp(suf)
    gain[2] = jnp.exp(pre + suf + ends[me_s, 1])
    gain[3] = norm

    @pl.loop(0, B - 1)
    def _(p):
        other = lo + (b + p + 1) % B

        def one_end(m, carry):
            pre, suf, between = carry
            end = ends[m, 1]
            pre = pre + jnp.where((m >= lo) & (m < other), 1.0, 0.0) * end
            suf = suf + jnp.where((m > other) & (m < hi), 1.0, 0.0) * end
            inside = (m > jnp.minimum(me_s, other)) & (m < jnp.maximum(me_s, other))
            between = between + jnp.where(inside, 1.0, 0.0) * end
            return (pre, suf, between)

        pre, suf, between = lax.fori_loop(0, S, one_end, (zero, zero, zero))
        zgain[p, 0] = jnp.exp(pre)
        zgain[p, 1] = jnp.where(other > me_s, 1.0, 0.0) * jnp.exp(between)
        zgain[p, 2] = jnp.exp(suf)
        zgain[p, 3] = jnp.where(other < me_s, 1.0, 0.0) * jnp.exp(between)

    def chain_copy(send, recv, ssem, rsem, m, target):
        return pltpu.make_async_remote_copy(
            src_ref=send.at[m],
            dst_ref=recv.at[m],
            send_sem=ssem.at[m],
            recv_sem=rsem.at[m],
            device_id={"seq": target},
            device_id_type=MESH,
        )

    def y_copy(m, target):
        return chain_copy(y_send, y_recv, y_ssem, y_rsem, m, target)

    def n_copy(m, target):
        return chain_copy(n_send, n_recv, n_ssem, n_rsem, m, target)

    def z_copy(send, recv, ssem, rsem, p, m, target):
        return pltpu.make_async_remote_copy(
            src_ref=send.at[p, m],
            dst_ref=recv.at[p, m],
            send_sem=ssem.at[p, m],
            recv_sem=rsem.at[p, m],
            device_id={"seq": target},
            device_id_type=MESH,
        )

    def zp_copy(p, m, target):
        return z_copy(zp_send, zp_recv, zp_ssem, zp_rsem, p, m, target)

    def zn_copy(p, m, target):
        return z_copy(zn_send, zn_recv, zn_ssem, zn_rsem, p, m, target)

    def peer(p):
        return lo + (b + p + 1) % B

    def source_peer(p):
        return lo + (b + B - p - 1) % B

    up = (me_s + B) % S
    down = (me_s + S - B) % S

    def weight(index, h):
        return gain[index, pl.ds(h, 1), :]

    def columns(h):
        return pl.ds(pl.multiple_of(h * DH, DH), DH)

    def arrive(m):
        for r in range(1, H):
            for t in range(4):
                a2a_copy(m, r, t, (me_h + H - r) % H, me_h).wait_recv()

    def states(m):
        for j in range(HC):
            h = m * HC + j
            at = columns(h)
            growth = grow[h]
            inverse = lax.rsqrt(growth * weight(3, h) + inner[h])
            inner[h] = inverse
            scaled = (rows[3, :, at].astype(F32) * inverse).astype(BF16)
            scaled_ref[h] = scaled
            key_fade = (rows[1, :, at].astype(F32) * fade[h]).astype(BF16)
            local[h] = dot_tn(key_fade, rows[2, :, at])
            query_growth = (rows[0, :, at].astype(F32) * growth).astype(BF16)
            reach[h] = dot_tn(query_growth, scaled)

    def within(m):
        for j in range(HC):
            h = m * HC + j
            at = columns(h)
            q, k, v, g = rows[0, :, at], rows[1, :, at], rows[2, :, at], rows[3, :, at]
            decay = table[h]
            weighted = (dot_nt(g, v) * decay * inner[h]).astype(BF16)
            affinity = (dot_nt(q, k) * decay).astype(BF16)
            part_q[h] = dot_nn(weighted, k)
            part_k[h] = dot_tn(weighted, q)
            part_v[h] = dot_tn(affinity, scaled_ref[h])

    def hop_up(m):
        @pl.when(a > 0)
        def _():
            y_copy(m, up).wait_recv()

        @pl.when(a < A - 1)
        def _():
            for j in range(HC):
                h = m * HC + j
                y_send[m, j] = (
                    weight(1, h) * local[h] + weight(2, h) * y_recv[m, j].astype(F32)
                ).astype(BF16)
            y_copy(m, up).start()

        @pl.loop(0, B - 1)
        def _(p):
            for j in range(HC):
                h = m * HC + j
                zp_send[p, m, j] = (
                    zgain[p, 0, pl.ds(h, 1), :] * y_recv[m, j].astype(F32)
                    + zgain[p, 1, pl.ds(h, 1), :] * local[h]
                ).astype(BF16)
            zp_copy(p, m, peer(p)).start()

    def hop_down(m):
        @pl.when(a < A - 1)
        def _():
            n_copy(m, down).wait_recv()

        @pl.when(a > 0)
        def _():
            for j in range(HC):
                h = m * HC + j
                n_send[m, j] = (
                    weight(0, h) * reach[h] + weight(2, h) * n_recv[m, j].astype(F32)
                ).astype(BF16)
            n_copy(m, down).start()

        @pl.loop(0, B - 1)
        def _(p):
            for j in range(HC):
                h = m * HC + j
                zn_send[p, m, j] = (
                    zgain[p, 2, pl.ds(h, 1), :] * n_recv[m, j].astype(F32)
                    + zgain[p, 3, pl.ds(h, 1), :] * reach[h]
                ).astype(BF16)
            zn_copy(p, m, peer(p)).start()

    def out_copy(t, m):
        at = pl.ds(pl.multiple_of(m * HC * DH, HC * DH), HC * DH)
        return pltpu.make_async_copy(
            out_rows.at[t, :, at], (gq_ref, gk_ref, gv_ref)[t].at[:, at], out_sem.at[t, m]
        )

    def finish(m):
        @pl.loop(0, B - 1)
        def _(p):
            zp_copy(p, m, source_peer(p)).wait_recv()
            zn_copy(p, m, source_peer(p)).wait_recv()

        for j in range(HC):
            h = m * HC + j
            at = columns(h)
            prefix = weight(0, h) * y_recv[m, j].astype(F32)
            later = weight(1, h) * n_recv[m, j].astype(F32)
            prefix, later = lax.fori_loop(
                0,
                B - 1,
                lambda p, both: (
                    both[0] + zp_recv[p, m, j].astype(F32),
                    both[1] + zn_recv[p, m, j].astype(F32),
                ),
                (prefix, later),
            )
            prefix, later = prefix.astype(BF16), later.astype(BF16)
            gq = part_q[h] + grow[h] * dot_nt(scaled_ref[h], prefix)
            gk = part_k[h] + fade[h] * dot_nt(rows[2, :, at], later)
            gv = part_v[h] + fade[h] * dot_nn(rows[1, :, at], later)
            out_rows[0, :, at] = gq.astype(BF16)
            out_rows[1, :, at] = gk.astype(BF16)
            out_rows[2, :, at] = gv.astype(BF16)
        for t in range(3):
            out_copy(t, m).start()

    def guarded(do, m):
        @pl.when((m >= 0) & (m < NC))
        def _():
            do(m)

    for t in range(4):
        own_copy(t).wait()

    @pl.loop(0, NC + LAG * (A - 1) + TAIL)
    def _(n):
        @pl.when((n < NC) & (n % PER == 0))
        def _():
            arrive(n // PER)

        @pl.when(n < NC)
        def _():
            states(n)

        guarded(hop_up, n - LAG * a)
        guarded(hop_down, n - LAG * (A - 1 - a))

        @pl.when(n < NC)
        def _():
            within(n)

        guarded(finish, n - LAG * (A - 1) - TAIL)

    @pl.loop(1, S)
    def _(r):
        end_copy(r, me_s, (me_s + r) % S).wait_send()

    @pl.loop(0, NH // ROW_HEADS)
    def _(m):
        for r in range(1, H):
            for t in range(4):
                a2a_copy(m, r, t, me_h, (me_h + r) % H).wait_send()

    @pl.loop(0, NC)
    def _(m):
        for t in range(3):
            out_copy(t, m).wait()

        @pl.when(a < A - 1)
        def _():
            y_copy(m, up).wait_send()

        @pl.when(a > 0)
        def _():
            n_copy(m, down).wait_send()

        @pl.loop(0, B - 1)
        def _(p):
            zp_copy(p, m, peer(p)).wait_send()
            zn_copy(p, m, peer(p)).wait_send()


def hand_over(x_ref, y_ref, z_ref, x_out, y_out, z_out):
    x_out[...] = x_ref[...]
    y_out[...] = y_ref[...]
    z_out[...] = z_ref[...]


def body(seq_size, head_size, queries, keys, values, grad_out, gates):
    S, H = seq_size, head_size
    B = S // SLOW
    RD, width = queries.shape
    T = RD * H
    CW = width // H
    NH = CW // DH
    HC = CHUNK_HEADS
    NC = NH // HC
    square = (NH, T, DH)
    state = (NH, DH, DH)
    message = (NC, HC, DH, DH)
    vmem = pltpu.VMEM
    dma = pltpu.SemaphoreType.DMA
    whole = pl.BlockSpec(memory_space=pltpu.VMEM)
    out = jax.ShapeDtypeStruct((T, CW), BF16)
    results = pl.pallas_call(
        functools.partial(kernel, S, H),
        out_shape=(out, out, out),
        in_specs=[pl.BlockSpec(memory_space=pl.ANY)] * 4 + [whole],
        out_specs=(pl.BlockSpec(memory_space=pl.ANY),) * 3,
        scratch_shapes=[
            vmem((4, T, CW), BF16),
            vmem((S, 2, NH, DH), F32),
            vmem((4, NH, DH), F32),
            vmem((NH, T, T), F32),
            vmem(square, F32),
            vmem(square, F32),
            vmem(square, F32),
            vmem(square, BF16),
            vmem(state, F32),
            vmem(state, F32),
            vmem(square, F32),
            vmem(square, F32),
            vmem(square, F32),
            vmem(message, BF16),
            vmem(message, BF16),
            vmem(message, BF16),
            vmem(message, BF16),
            vmem((B - 1,) + message, BF16),
            vmem((B - 1,) + message, BF16),
            vmem((B - 1,) + message, BF16),
            vmem((B - 1,) + message, BF16),
            vmem((B - 1, 4, NH, DH), F32),
            vmem((3, T, CW), BF16),
            vmem((4, RD, width), BF16),
            dma((4,)),
            dma((3, NC)),
            dma((4,)),
            dma((NH // ROW_HEADS, H - 1, 4)),
            dma((NH // ROW_HEADS, H - 1, 4)),
            dma((S - 1,)),
            dma((S - 1,)),
            dma((NC,)),
            dma((NC,)),
            dma((NC,)),
            dma((NC,)),
            dma((B - 1, NC)),
            dma((B - 1, NC)),
            dma((B - 1, NC)),
            dma((B - 1, NC)),
        ],
        compiler_params=pltpu.CompilerParams(
            collective_id=0,
            has_side_effects=True,
            vmem_limit_bytes=60 << 20,
        ),
    )(queries, keys, values, grad_out, gates.T)
    return pl.pallas_call(
        hand_over,
        out_shape=(out, out, out),
        in_specs=[whole] * 3,
        out_specs=(whole, whole, whole),
        compiler_params=pltpu.CompilerParams(vmem_limit_bytes=60 << 20),
    )(*results)


def solution(mesh):
    placed = (
        P(("seq", "head"), None),
        P(("seq", "head"), None),
        P(("seq", "head"), None),
        P(("seq", "head"), None),
        P("seq", "head"),
    )
    return jax.shard_map(
        functools.partial(body, mesh.shape["seq"], mesh.shape["head"]),
        mesh=mesh,
        in_specs=placed,
        out_specs=(P("seq", "head"), P("seq", "head"), P("seq", "head")),
        check_vma=False,
    )
```

```python
import functools

import jax
import jax.numpy as jnp
from jax import lax
from jax.experimental import pallas as pl
from jax.experimental.pallas import tpu as pltpu
from jax.sharding import PartitionSpec as P

HEAD_COUNT = 32
DH = 128
SLOW = 4
ROW_HEADS = 2
CHUNK_HEADS = 1
LAG = 2
SPREAD = 1
TAIL = 3

MESH = pl.DeviceIdType.MESH
F32 = jnp.float32
BF16 = jnp.bfloat16
EXACT = lax.Precision.HIGHEST


def dot_nn(x, y):
    return lax.dot_general(x, y, (((1,), (0,)), ((), ())), preferred_element_type=F32)


def dot_nt(x, y):
    return lax.dot_general(x, y, (((1,), (1,)), ((), ())), preferred_element_type=F32)


def dot_tn(x, y):
    return lax.dot_general(x, y, (((0,), (0,)), ((), ())), preferred_element_type=F32)


def kernel(
    seq_size, head_size,
    q_ref, k_ref, v_ref, g_ref, gates_ref,
    gq_ref, gk_ref, gv_ref,
    rows, ends, gain, table, grow, fade, inner, scaled_ref,
    local, reach, part_q, part_k, part_v,
    y_send, y_recv, n_send, n_recv, zp_send, zp_recv, zn_send, zn_recv,
    zgain, out_rows, staged, dy_recv, dn_recv, sum_p, sum_n,
    dy_ssem, dy_rsem, dn_ssem, dn_rsem,
    in_sem, out_sem, own_sem, a2a_ssem, a2a_rsem, end_ssem, end_rsem,
    y_ssem, y_rsem, n_ssem, n_rsem, zp_ssem, zp_rsem, zn_ssem, zn_rsem,
):
    S, H = seq_size, head_size
    A = SLOW
    B = S // A
    RD = q_ref.shape[0]
    T = RD * H
    CW = q_ref.shape[1] // H
    NH = CW // DH
    HC = CHUNK_HEADS
    NC = NH // HC
    first = NC - SPREAD
    RC = ROW_HEADS * DH
    PER = ROW_HEADS // HC
    me_s = lax.axis_index("seq")
    me_h = lax.axis_index("head")
    a = me_s // B
    b = me_s % B
    lo = a * B
    hi = lo + B

    def in_copy(t):
        return pltpu.make_async_copy(
            (q_ref, k_ref, v_ref, g_ref)[t], staged.at[t], in_sem.at[t]
        )

    for t in range(4):
        in_copy(t).start()

    barrier = pltpu.get_barrier_semaphore()
    for r in range(1, H):
        pl.semaphore_signal(
            barrier, inc=1, device_id={"head": (me_h + r) % H}, device_id_type=MESH
        )

    @pl.loop(1, S)
    def _(r):
        pl.semaphore_signal(
            barrier, inc=1, device_id={"seq": (me_s + r) % S}, device_id_type=MESH
        )

    pl.semaphore_wait(barrier, (H - 1) + (S - 1))

    def a2a_copy(ch, r, t, source, target):
        return pltpu.make_async_remote_copy(
            src_ref=staged.at[t, :, pl.ds(pl.multiple_of(target * CW + ch * RC, RC), RC)],
            dst_ref=rows.at[
                t,
                pl.ds(pl.multiple_of(source * RD, RD), RD),
                pl.ds(pl.multiple_of(ch * RC, RC), RC),
            ],
            send_sem=a2a_ssem.at[ch, r - 1, t],
            recv_sem=a2a_rsem.at[ch, r - 1, t],
            device_id={"head": target},
            device_id_type=MESH,
        )

    for t in range(4):
        in_copy(t).wait()

    def send_rows(ch):
        for t in (1, 2, 0, 3):
            for r in range(1, H):
                a2a_copy(ch, r, t, me_h, (me_h + r) % H).start()

    send_rows(0)

    t_at = lax.broadcasted_iota(jnp.int32, (T, T), 0)
    s_at = lax.broadcasted_iota(jnp.int32, (T, T), 1)
    causal = t_at >= s_at
    tri = jnp.where(causal, 1.0, 0.0).astype(F32)
    c_row = lax.dot_general(
        gates_ref[...], tri, (((1,), (1,)), ((), ())), precision=EXACT, preferred_element_type=F32
    )
    c_col = c_row.T
    e_col = c_row[:, T - 1 : T]
    norm_col = jnp.sum(jnp.exp(e_col - c_row), axis=1, keepdims=True)
    ends[me_s, 0] = jnp.broadcast_to(norm_col, (NH, DH))
    ends[me_s, 1] = jnp.broadcast_to(e_col, (NH, DH))

    def end_copy(r, source, target):
        return pltpu.make_async_remote_copy(
            src_ref=ends.at[source],
            dst_ref=ends.at[source],
            send_sem=end_ssem.at[r - 1],
            recv_sem=end_rsem.at[r - 1],
            device_id={"seq": target},
            device_id_type=MESH,
        )

    @pl.loop(1, S)
    def _(r):
        end_copy(r, me_s, (me_s + r) % S).start()


    @pl.loop(1, NH // ROW_HEADS)
    def _(ch):
        send_rows(ch)

    own_rows = pl.ds(pl.multiple_of(me_h * RD, RD), RD)
    own_cols = pl.ds(pl.multiple_of(me_h * CW, CW), CW)
    def own_copy(t):
        return pltpu.make_async_copy(
            staged.at[t, :, own_cols], rows.at[t, own_rows, :], own_sem.at[t]
        )

    for t in range(4):
        own_copy(t).start()

    @pl.when(a == 0)
    def _():
        y_recv[...] = jnp.zeros_like(y_recv)
        dy_recv[...] = jnp.zeros_like(dy_recv)

    @pl.when(a == A - 1)
    def _():
        n_recv[...] = jnp.zeros_like(n_recv)
        dn_recv[...] = jnp.zeros_like(dn_recv)

    for h in range(NH):
        col = c_col[:, h : h + 1]
        row = c_row[h : h + 1, :]
        decay = jnp.where(causal, jnp.exp(jnp.where(causal, col - row, 0.0)), 0.0)
        table[h] = decay
        grow[h] = jnp.broadcast_to(jnp.exp(col), (T, DH))
        fade[h] = jnp.broadcast_to(jnp.exp(c_col[T - 1 : T, h : h + 1] - col), (T, DH))
        inner[h] = jnp.broadcast_to(jnp.sum(decay, axis=1, keepdims=True), (T, DH))

    @pl.loop(1, S)
    def _(r):
        end_copy(r, (me_s + S - r) % S, me_s).wait_recv()

    zero = jnp.zeros((NH, DH), F32)

    def one_block(m, carry):
        pre, suf, norm = carry
        end = ends[m, 1]
        pre = pre + jnp.where((m >= lo) & (m < me_s), 1.0, 0.0) * end
        suf = suf + jnp.where((m > me_s) & (m < hi), 1.0, 0.0) * end
        earlier = jnp.where(m < me_s, 1.0, 0.0)
        norm = earlier * (norm * jnp.exp(end) + ends[m, 0]) + (1.0 - earlier) * norm
        return (pre, suf, norm)

    pre, suf, norm = lax.fori_loop(0, S, one_block, (zero, zero, zero))
    gain[0] = jnp.exp(pre)
    gain[1] = jnp.exp(suf)
    gain[2] = jnp.exp(pre + suf + ends[me_s, 1])
    gain[3] = norm

    @pl.loop(0, B - 1)
    def _(p):
        other = lo + (b + p + 1) % B

        def one_end(m, carry):
            pre, suf, between = carry
            end = ends[m, 1]
            pre = pre + jnp.where((m >= lo) & (m < other), 1.0, 0.0) * end
            suf = suf + jnp.where((m > other) & (m < hi), 1.0, 0.0) * end
            inside = (m > jnp.minimum(me_s, other)) & (m < jnp.maximum(me_s, other))
            between = between + jnp.where(inside, 1.0, 0.0) * end
            return (pre, suf, between)

        pre, suf, between = lax.fori_loop(0, S, one_end, (zero, zero, zero))
        zgain[p, 0] = jnp.exp(pre)
        zgain[p, 1] = jnp.where(other > me_s, 1.0, 0.0) * jnp.exp(between)
        zgain[p, 2] = jnp.exp(suf)
        zgain[p, 3] = jnp.where(other < me_s, 1.0, 0.0) * jnp.exp(between)

    def chain_copy(send, recv, ssem, rsem, m, target):
        return pltpu.make_async_remote_copy(
            src_ref=send.at[m],
            dst_ref=recv.at[m],
            send_sem=ssem.at[m],
            recv_sem=rsem.at[m],
            device_id={"seq": target},
            device_id_type=MESH,
        )

    def y_copy(m, target):
        return chain_copy(y_send, y_recv, y_ssem, y_rsem, m, target)

    def n_copy(m, target):
        return chain_copy(n_send, n_recv, n_ssem, n_rsem, m, target)

    def z_copy(send, recv, ssem, rsem, p, m, target):
        return pltpu.make_async_remote_copy(
            src_ref=send.at[p, m],
            dst_ref=recv.at[p, m],
            send_sem=ssem.at[p, m],
            recv_sem=rsem.at[p, m],
            device_id={"seq": target},
            device_id_type=MESH,
        )

    def zp_copy(p, m, target):
        return z_copy(zp_send, zp_recv, zp_ssem, zp_rsem, p, m, target)

    def zn_copy(p, m, target):
        return z_copy(zn_send, zn_recv, zn_ssem, zn_rsem, p, m, target)

    def spread_copy(send, recv, ssem, rsem, p, m, target):
        return pltpu.make_async_remote_copy(
            src_ref=send.at[m],
            dst_ref=recv.at[p, m - first],
            send_sem=ssem.at[p, m - first],
            recv_sem=rsem.at[p, m - first],
            device_id={"seq": target},
            device_id_type=MESH,
        )

    def dy_copy(p, m):
        target = (peer(p) + B) % S
        return spread_copy(y_send, dy_recv, dy_ssem, dy_rsem, p, m, target)

    def dn_copy(p, m):
        target = (peer(p) + S - B) % S
        return spread_copy(n_send, dn_recv, dn_ssem, dn_rsem, p, m, target)

    def peer(p):
        return lo + (b + p + 1) % B

    def source_peer(p):
        return lo + (b + B - p - 1) % B

    up = (me_s + B) % S
    down = (me_s + S - B) % S

    def weight(index, h):
        return gain[index, pl.ds(h, 1), :]

    def columns(h):
        return pl.ds(pl.multiple_of(h * DH, DH), DH)

    def arrive(m):
        for r in range(1, H):
            for t in range(4):
                a2a_copy(m, r, t, (me_h + H - r) % H, me_h).wait_recv()

    def states(m):
        for j in range(HC):
            h = m * HC + j
            at = columns(h)
            growth = grow[h]
            inverse = lax.rsqrt(growth * weight(3, h) + inner[h])
            inner[h] = inverse
            scaled = (rows[3, :, at].astype(F32) * inverse).astype(BF16)
            scaled_ref[h] = scaled
            key_fade = (rows[1, :, at].astype(F32) * fade[h]).astype(BF16)
            local[h] = dot_tn(key_fade, rows[2, :, at])
            query_growth = (rows[0, :, at].astype(F32) * growth).astype(BF16)
            reach[h] = dot_tn(query_growth, scaled)

    def within(m):
        for j in range(HC):
            h = m * HC + j
            at = columns(h)
            q, k, v, g = rows[0, :, at], rows[1, :, at], rows[2, :, at], rows[3, :, at]
            decay = table[h]
            weighted = (dot_nt(g, v) * decay * inner[h]).astype(BF16)
            affinity = (dot_nt(q, k) * decay).astype(BF16)
            part_q[h] = dot_nn(weighted, k)
            part_k[h] = dot_tn(weighted, q)
            part_v[h] = dot_tn(affinity, scaled_ref[h])

    def early(m):
        @pl.loop(0, B - 1)
        def _(p):
            for j in range(HC):
                h = m * HC + j
                zp_send[p, m, j] = (zgain[p, 1, pl.ds(h, 1), :] * local[h]).astype(BF16)
                zn_send[p, m, j] = (zgain[p, 3, pl.ds(h, 1), :] * reach[h]).astype(BF16)
            zp_copy(p, m, peer(p)).start()
            zn_copy(p, m, peer(p)).start()

    def hop_up(m):
        @pl.when(a > 0)
        def _():
            y_copy(m, up).wait_recv()

        @pl.when(a < A - 1)
        def _():
            for j in range(HC):
                h = m * HC + j
                y_send[m, j] = (
                    weight(1, h) * local[h] + weight(2, h) * y_recv[m, j].astype(F32)
                ).astype(BF16)
            y_copy(m, up).start()

            @pl.when(m >= first)
            def _():
                @pl.loop(0, B - 1)
                def _(p):
                    dy_copy(p, m).start()

        @pl.loop(0, jnp.where(m < first, B - 1, 0))
        def _(p):
            for j in range(HC):
                h = m * HC + j
                zp_send[p, m, j] = (
                    zgain[p, 0, pl.ds(h, 1), :] * y_recv[m, j].astype(F32)
                    + zgain[p, 1, pl.ds(h, 1), :] * local[h]
                ).astype(BF16)
            zp_copy(p, m, peer(p)).start()

    def hop_down(m):
        @pl.when(a < A - 1)
        def _():
            n_copy(m, down).wait_recv()

        @pl.when(a > 0)
        def _():
            for j in range(HC):
                h = m * HC + j
                n_send[m, j] = (
                    weight(0, h) * reach[h] + weight(2, h) * n_recv[m, j].astype(F32)
                ).astype(BF16)
            n_copy(m, down).start()

            @pl.when(m >= first)
            def _():
                @pl.loop(0, B - 1)
                def _(p):
                    dn_copy(p, m).start()

        @pl.loop(0, jnp.where(m < first, B - 1, 0))
        def _(p):
            for j in range(HC):
                h = m * HC + j
                zn_send[p, m, j] = (
                    zgain[p, 2, pl.ds(h, 1), :] * n_recv[m, j].astype(F32)
                    + zgain[p, 3, pl.ds(h, 1), :] * reach[h]
                ).astype(BF16)
            zn_copy(p, m, peer(p)).start()

    def out_copy(t, m):
        at = pl.ds(pl.multiple_of(m * HC * DH, HC * DH), HC * DH)
        return pltpu.make_async_copy(
            out_rows.at[t, :, at], (gq_ref, gk_ref, gv_ref)[t].at[:, at], out_sem.at[t, m]
        )

    def finish(m):
        @pl.loop(0, B - 1)
        def _(p):
            zp_copy(p, m, source_peer(p)).wait_recv()
            zn_copy(p, m, source_peer(p)).wait_recv()

        for j in range(HC):
            sum_p[j] = y_recv[m, j].astype(F32)
            sum_n[j] = n_recv[m, j].astype(F32)

        @pl.when(m >= first)
        def _():
            @pl.loop(0, B - 1)
            def _(p):
                @pl.when(a > 0)
                def _():
                    dy_copy(p, m).wait_recv()

                @pl.when(a < A - 1)
                def _():
                    dn_copy(p, m).wait_recv()

                for j in range(HC):
                    sum_p[j] += dy_recv[p, m - first, j].astype(F32)
                    sum_n[j] += dn_recv[p, m - first, j].astype(F32)

        for j in range(HC):
            h = m * HC + j
            at = columns(h)
            prefix = weight(0, h) * sum_p[j]
            later = weight(1, h) * sum_n[j]
            prefix, later = lax.fori_loop(
                0,
                B - 1,
                lambda p, both: (
                    both[0] + zp_recv[p, m, j].astype(F32),
                    both[1] + zn_recv[p, m, j].astype(F32),
                ),
                (prefix, later),
            )
            prefix, later = prefix.astype(BF16), later.astype(BF16)
            gq = part_q[h] + grow[h] * dot_nt(scaled_ref[h], prefix)
            gk = part_k[h] + fade[h] * dot_nt(rows[2, :, at], later)
            gv = part_v[h] + fade[h] * dot_nn(rows[1, :, at], later)
            out_rows[0, :, at] = gq.astype(BF16)
            out_rows[1, :, at] = gk.astype(BF16)
            out_rows[2, :, at] = gv.astype(BF16)
        for t in range(3):
            out_copy(t, m).start()

    def guarded(do, m):
        @pl.when((m >= 0) & (m < NC))
        def _():
            do(m)

    for t in range(4):
        own_copy(t).wait()

    @pl.loop(0, NC + LAG * (A - 1) + TAIL)
    def _(n):
        @pl.when((n < NC) & (n % PER == 0))
        def _():
            arrive(n // PER)

        @pl.when(n < NC)
        def _():
            states(n)

        @pl.when((n >= first) & (n < NC))
        def _():
            early(n)

        guarded(hop_up, n - LAG * a)
        guarded(hop_down, n - LAG * (A - 1 - a))

        @pl.when(n < NC)
        def _():
            within(n)

        guarded(finish, n - LAG * (A - 1) - TAIL)

    @pl.loop(1, S)
    def _(r):
        end_copy(r, me_s, (me_s + r) % S).wait_send()

    @pl.loop(0, NH // ROW_HEADS)
    def _(m):
        for r in range(1, H):
            for t in range(4):
                a2a_copy(m, r, t, me_h, (me_h + r) % H).wait_send()

    @pl.loop(0, NC)
    def _(m):
        for t in range(3):
            out_copy(t, m).wait()

        @pl.when(a < A - 1)
        def _():
            y_copy(m, up).wait_send()

        @pl.when(a > 0)
        def _():
            n_copy(m, down).wait_send()

        @pl.when(m >= first)
        def _():
            @pl.loop(0, B - 1)
            def _(p):
                @pl.when(a < A - 1)
                def _():
                    dy_copy(p, m).wait_send()

                @pl.when(a > 0)
                def _():
                    dn_copy(p, m).wait_send()

        @pl.loop(0, B - 1)
        def _(p):
            zp_copy(p, m, peer(p)).wait_send()
            zn_copy(p, m, peer(p)).wait_send()


def hand_over(x_ref, y_ref, z_ref, x_out, y_out, z_out, held, in_sems, out_sems):
    sources, targets = (x_ref, y_ref, z_ref), (x_out, y_out, z_out)
    loads = [pltpu.make_async_copy(sources[i], held.at[i], in_sems.at[i]) for i in range(3)]
    stores = [pltpu.make_async_copy(held.at[i], targets[i], out_sems.at[i]) for i in range(3)]
    for load in loads:
        load.start()
    for load, store in zip(loads, stores):
        load.wait()
        store.start()
    for store in stores:
        store.wait()


def body(seq_size, head_size, queries, keys, values, grad_out, gates):
    S, H = seq_size, head_size
    B = S // SLOW
    RD, width = queries.shape
    T = RD * H
    CW = width // H
    NH = CW // DH
    HC = CHUNK_HEADS
    NC = NH // HC
    square = (NH, T, DH)
    state = (NH, DH, DH)
    message = (NC, HC, DH, DH)
    vmem = pltpu.VMEM
    dma = pltpu.SemaphoreType.DMA
    whole = pl.BlockSpec(memory_space=pltpu.VMEM)
    out = jax.ShapeDtypeStruct((T, CW), BF16)
    results = pl.pallas_call(
        functools.partial(kernel, S, H),
        out_shape=(out, out, out),
        in_specs=[pl.BlockSpec(memory_space=pl.ANY)] * 4 + [whole],
        out_specs=(pl.BlockSpec(memory_space=pl.ANY),) * 3,
        scratch_shapes=[
            vmem((4, T, CW), BF16),
            vmem((S, 2, NH, DH), F32),
            vmem((4, NH, DH), F32),
            vmem((NH, T, T), F32),
            vmem(square, F32),
            vmem(square, F32),
            vmem(square, F32),
            vmem(square, BF16),
            vmem(state, F32),
            vmem(state, F32),
            vmem(square, F32),
            vmem(square, F32),
            vmem(square, F32),
            vmem(message, BF16),
            vmem(message, BF16),
            vmem(message, BF16),
            vmem(message, BF16),
            vmem((B - 1,) + message, BF16),
            vmem((B - 1,) + message, BF16),
            vmem((B - 1,) + message, BF16),
            vmem((B - 1,) + message, BF16),
            vmem((B - 1, 4, NH, DH), F32),
            vmem((3, T, CW), BF16),
            vmem((4, RD, width), BF16),
            vmem((B - 1, SPREAD, HC, DH, DH), BF16),
            vmem((B - 1, SPREAD, HC, DH, DH), BF16),
            vmem((HC, DH, DH), F32),
            vmem((HC, DH, DH), F32),
            dma((B - 1, SPREAD)),
            dma((B - 1, SPREAD)),
            dma((B - 1, SPREAD)),
            dma((B - 1, SPREAD)),
            dma((4,)),
            dma((3, NC)),
            dma((4,)),
            dma((NH // ROW_HEADS, H - 1, 4)),
            dma((NH // ROW_HEADS, H - 1, 4)),
            dma((S - 1,)),
            dma((S - 1,)),
            dma((NC,)),
            dma((NC,)),
            dma((NC,)),
            dma((NC,)),
            dma((B - 1, NC)),
            dma((B - 1, NC)),
            dma((B - 1, NC)),
            dma((B - 1, NC)),
        ],
        compiler_params=pltpu.CompilerParams(
            collective_id=0,
            has_side_effects=True,
            vmem_limit_bytes=60 << 20,
        ),
    )(queries, keys, values, grad_out, gates.T)
    return pl.pallas_call(
        hand_over,
        out_shape=(out, out, out),
        in_specs=[pl.BlockSpec(memory_space=pl.ANY)] * 3,
        out_specs=(pl.BlockSpec(memory_space=pl.ANY),) * 3,
        scratch_shapes=[vmem((3, T, CW), BF16), dma((3,)), dma((3,))],
        compiler_params=pltpu.CompilerParams(vmem_limit_bytes=60 << 20),
    )(*results)


def solution(mesh):
    placed = (
        P(("seq", "head"), None),
        P(("seq", "head"), None),
        P(("seq", "head"), None),
        P(("seq", "head"), None),
        P("seq", "head"),
    )
    return jax.shard_map(
        functools.partial(body, mesh.shape["seq"], mesh.shape["head"]),
        mesh=mesh,
        in_specs=placed,
        out_specs=(P("seq", "head"), P("seq", "head"), P("seq", "head")),
        check_vma=False,
    )
```
